512 devices in a mesh: seq: 64 (over x, y, core), expert: 8 (over z).
Axes of the slice: x: 4, y: 8, z: 8, core: 2. Of those that a mesh axis runs over, the one named last changes fastest.
Arguments:
- new_q: bfloat16 [64, 4, 1024], P('expert'), may hold values from -12 to 12
- new_k: bfloat16 [64, 4, 1024], P('expert'), may hold values from -12 to 12
- new_v: bfloat16 [64, 4, 1024], P('expert'), may hold values from -6 to 6
- k_cache: bfloat16 [8, 256, 128, 1024], P('expert', 'seq'), may hold values from -8 to 8
- v_cache: bfloat16 [8, 256, 128, 1024], P('expert', 'seq'), may hold values from -6 to 6
- lengths: int32 [64], P('expert'), may hold values from 4097 to 16384, as said below
- prompt_group: int32 [64], P('expert'), may hold values from 0 to 15, as said below
- prefix_table: int32 [16, 32], P('expert'), may hold values from 0 to 255, as said below
- page_table: int32 [64, 96], P('expert'), may hold values from -1 to 255, as said below
- rel_bucket: int32 [16388], replicated, may hold values from 0 to 31, as said below
- bias_table: float32 [32, 16], replicated, may hold values from -8 to 8
- hidden_in: bfloat16 [64, 4, 1024], P('expert', None, 'seq'), may hold values from -600 to 600
- out_proj: bfloat16 [1024, 1024], P(None, 'seq'), may hold values from -0.1875 to 0.1875
- norm_gain: float32 [1024], P('seq'), may hold values from 0.1 to 1.9
- router_w: float32 [1024, 16], P('seq'), may hold values from -0.1875 to 0.1875
- expert_ids: int32 [64, 4, 2], P('expert'), may hold values from 0 to 15, all different within a row; in each aligned block of 32 rows (0 to 31, 32 to 63, ..., all dimensions but the last counted through in order) at most 8 rows name the same one
- w_in: bfloat16 [16, 1024, 2, 2816], P('expert', None, None, 'seq'), may hold values from -0.1875 to 0.1875
- w_down: bfloat16 [16, 2816, 1024], P('expert', 'seq'), may hold values from -0.109375 to 0.109375
Outputs:
- attn_out: bfloat16 [64, 4, 1024], P('expert', None, 'seq')
- moe_out: bfloat16 [64, 4, 1024], P('expert', None, 'seq')
The draws below stay inside these ranges and needn't reach their ends.
Inputs may be any that keep to these rules, and one draw needn't show every extreme that they name: `lengths`: at least 4097; in every block of 8 requests one request has exactly 16384. `prompt_group`: the groups of block b are b * 2 to b * 2 + 1, each holding 8 // 2 requests of that block. `prefix_table`: pages of the pool of the group's block. Entry j is -1 exactly when j * 128 is at least the request's own tokens, lengths - 4096. Within one block no pool page appears twice across prefix_table and page_table. `rel_bucket`: equal to the distance below 16; never falls as the distance grows. `expert_ids`: in the 32 rows of one block no expert is named more than 8 times.
All inputs are finite; a program needn't handle non-finite values.
Results may differ from the reference program's by a relative error of at most 0.014.
Values may be sent and summed in bfloat16 or wider, within the bound.
No kernel may reach another device: no remote copies, remote signals or barrier semaphores. Data moves between devices by JAX's collectives and lax.ppermute only.
A program may use at most 64 MiB of HBM per device.

```python
import math
import jax
import jax.numpy as jnp
import numpy as np
from jax import lax

D = 1024
H = 16
HD = 64
FF = 2816
EXPERTS = 16
TOP = 2
BUCKETS = 32
PAGE = 128
STEPS = 4
G_DEV = 2
REQ_DEV = 8
POOL = 256
POOLS = 8
PREFIX_PAGES = 32
LONGEST = 96
MAX_LEN = 16384
MAX_DIST = 16388
REQS = 64
MOST = 8
N_EXPERT = 8


def pool_layout(key):
    subkeys = jax.random.split(key, 5)
    longest = jax.random.randint(subkeys[0], (), 0, REQ_DEV)
    cut_order = jax.random.permutation(subkeys[1], LONGEST - 1).astype(jnp.int32) + 1
    cut_points = jnp.sort(cut_order[:REQ_DEV - 2])
    bounds = jnp.concatenate([jnp.zeros((1,), jnp.int32), cut_points, jnp.full((1,), LONGEST, jnp.int32)])
    page_parts = bounds[1:] - bounds[:-1]
    requests = jnp.arange(REQ_DEV, dtype=jnp.int32)
    other_index = jnp.clip(requests - (requests > longest).astype(jnp.int32), 0, REQ_DEV - 2)
    own_pages = jnp.where(requests == longest, LONGEST, page_parts[other_index]).astype(jnp.int32)
    trimmed = jax.random.randint(subkeys[2], (REQ_DEV,), 0, PAGE)
    trimmed = jnp.where(requests == longest, 0, trimmed)
    lengths = (PREFIX_PAGES * PAGE + own_pages * PAGE - trimmed).astype(jnp.int32)
    pool_order = jax.random.permutation(subkeys[3], POOL).astype(jnp.int32)
    prefix = pool_order[:G_DEV * PREFIX_PAGES].reshape(G_DEV, PREFIX_PAGES)
    starts = jnp.cumsum(own_pages) - own_pages
    column = jnp.arange(LONGEST, dtype=jnp.int32)
    slot_index = G_DEV * PREFIX_PAGES + starts[:, None] + column[None, :]
    page_rows = jnp.where(column[None, :] < own_pages[:, None], pool_order[jnp.clip(slot_index, 0, POOL - 1)], -1)
    shuffled = jax.random.permutation(subkeys[4], REQ_DEV).astype(jnp.int32)
    groups = shuffled // (REQ_DEV // G_DEV)
    return (lengths, page_rows.astype(jnp.int32), prefix, groups)


def all_pools(key):
    pool_keys = jax.random.split(jax.random.fold_in(key, 7), POOLS)
    lengths, page_rows, prefix, groups = jax.vmap(pool_layout)(pool_keys)
    offsets = (jnp.arange(POOLS, dtype=jnp.int32) * G_DEV)[:, None]
    return (lengths.reshape(-1), page_rows.reshape(-1, LONGEST), prefix.reshape(-1, PREFIX_PAGES), (groups + offsets).reshape(-1))


def draw_lengths(key, part):
    return all_pools(key)[0]


def draw_page_table(key, part):
    return all_pools(key)[1]


def draw_prefix_table(key, part):
    return all_pools(key)[2]


def draw_prompt_group(key, part):
    return all_pools(key)[3]


def draw_rel_bucket(key, part):
    exact = BUCKETS // 2
    spots = jax.random.permutation(jax.random.fold_in(key, 5), MAX_DIST - exact)[:BUCKETS - exact].astype(jnp.int32) + exact
    distance = jnp.arange(MAX_DIST, dtype=jnp.int32)
    far_bucket = exact - 1 + jnp.sum((distance[:, None] >= spots[None, :]).astype(jnp.int32), axis=1)
    return jnp.where(distance < exact, distance, far_bucket).astype(jnp.int32)


def aligned(key):
    sign_key = jax.random.fold_in(key, 11)
    signs = jnp.where(jax.random.bernoulli(sign_key, 0.5, (REQS, D)), 1.0, -1.0).astype(jnp.float32)
    request_ids = jnp.arange(REQS)
    picked = request_ids % 8 == 3
    target = jnp.array([110.0, 160.0, 230.0], jnp.float32)[request_ids // 8 % 3]
    strength = jnp.sqrt(target / math.sqrt(HD))
    return (picked, strength, signs * strength[:, None])


def cache_aligned(key):
    sign_key = jax.random.fold_in(key, 13)
    signs = jnp.where(jax.random.bernoulli(sign_key, 0.5, (REQS, D)), 1.0, -1.0).astype(jnp.float32)
    request_ids = jnp.arange(REQS, dtype=jnp.int32)
    picked = request_ids % REQ_DEV == 0
    target = jnp.array([150.0, 200.0, 240.0], jnp.float32)[request_ids // REQ_DEV % 3]
    strength = jnp.sqrt(target / math.sqrt(HD))
    pattern = signs * strength[:, None]
    head_lead = jnp.arange(D) % HD == 0
    shrink = 1.0 - 2.0 * math.sqrt(HD) / (strength[:, None] * strength[:, None])
    nudged = jnp.where(head_lead[None, :], pattern * shrink, pattern)
    return (picked, pattern, nudged)


def draw_new_q(key, part):
    drawn = jax.random.normal(jax.random.fold_in(key, 1), (REQS, STEPS, D), jnp.float32)
    picked, strength, pattern = aligned(key)
    last_step = (jnp.arange(STEPS) == STEPS - 1)[None, :, None]
    drawn = jnp.where(picked[:, None, None] & last_step, pattern[:, None, :], drawn)
    cache_picked, cache_pattern, cache_nudged = cache_aligned(key)
    first_step = (jnp.arange(STEPS) == 0)[None, :, None]
    drawn = jnp.where(cache_picked[:, None, None] & first_step, cache_pattern[:, None, :], drawn)
    return jnp.clip(drawn, -12.0, 12.0).astype(jnp.bfloat16)


def draw_new_k(key, part):
    drawn = jax.random.normal(jax.random.fold_in(key, 2), (REQS, STEPS, D), jnp.float32)
    picked, strength, pattern = aligned(key)
    head_lead = jnp.arange(D) % HD == 0
    shrink = 1.0 - 2.0 * math.sqrt(HD) / (strength[:, None] * strength[:, None])
    nudged = jnp.where(head_lead[None, :], pattern * shrink, pattern)
    first_step = (jnp.arange(STEPS) == 0)[None, :, None]
    second_step = (jnp.arange(STEPS) == 1)[None, :, None]
    drawn = jnp.where(picked[:, None, None] & first_step, pattern[:, None, :], drawn)
    drawn = jnp.where(picked[:, None, None] & second_step, nudged[:, None, :], drawn)
    return jnp.clip(drawn, -12.0, 12.0).astype(jnp.bfloat16)


def draw_k_cache(key, part):
    shape = (POOLS, POOL, PAGE, D)
    drawn = jnp.clip(jax.random.normal(jax.random.fold_in(key, 8), shape, jnp.float32), -6.0, 6.0)
    lengths, page_rows, prefix, groups = all_pools(key)
    pool_ids = jnp.arange(POOLS, dtype=jnp.int32)
    firsts = pool_ids * REQ_DEV
    first_pages = prefix[groups[firsts], 0].astype(jnp.int32)
    cache_picked, cache_pattern, cache_nudged = cache_aligned(key)
    drawn = drawn.at[pool_ids, first_pages, 0].set(cache_pattern[firsts])
    drawn = drawn.at[pool_ids, first_pages, 1].set(cache_nudged[firsts])
    return jnp.clip(drawn, -8.0, 8.0).astype(jnp.bfloat16)


def draw_hidden_in(key, part):
    columns = jnp.exp(jnp.arange(D, dtype=jnp.float32) / D * math.log(10.0))
    row_scale = jnp.exp(jax.random.uniform(jax.random.fold_in(key, 3), (REQS, STEPS, 1), jnp.float32, 0.0, math.log(10.0)))
    noise = jnp.clip(jax.random.normal(jax.random.fold_in(key, 4), (REQS, STEPS, D), jnp.float32), -6.0, 6.0)
    return (noise * columns * row_scale).astype(jnp.bfloat16)


def levels(own_key, extent, shards, least, high):
    loudness = 1.0
    for axis_at, shards_of in shards:
        heights = jax.random.uniform(jax.random.fold_in(jax.random.fold_in(own_key, 6), axis_at), (shards_of,), jnp.float32, least / len(shards), high / len(shards))
        loudness = loudness * jnp.repeat(jnp.exp(heights), extent[axis_at] // shards_of).reshape((-1,) + (1,) * (len(extent) - 1 - axis_at))
    return loudness


def assign_block(key, own, number, rows, amount, top, reach, skew):
    ranking = jax.random.permutation(key, amount)
    packed, usual = portions_of(amount, rows * top, reach, skew, True), portions_of(amount, rows * top, reach, skew, False)
    places = jnp.arange(amount)

    def named(sizes, turn):
        used = int((sizes > 0).sum())
        fixed = max(1, used // 4)
        passed = fixed + (places - fixed + turn * (used - fixed)) % max(1, amount - fixed)
        return jnp.zeros((amount,), jnp.int32).at[ranking[jnp.where(places < fixed, places, passed)]].set(jnp.asarray(sizes, jnp.int32))

    sizes = jnp.where(number % 4 == 0, named(packed, number // 4), named(usual, number - number // 4 - 1))
    mixed = jax.random.permutation(jax.random.fold_in(own, 3), amount)
    giver, receiver = mixed[0:amount // 2 * 2:2], mixed[1:amount // 2 * 2:2]
    slack = jnp.minimum(sizes[giver] - 1, reach - sizes[receiver]) // 2
    slack = jnp.where((giver == ranking[0]) | (receiver == ranking[0]) | (sizes[receiver] == 0), 0, jnp.maximum(slack, 0))
    passed = jax.random.randint(jax.random.fold_in(own, 4), (amount // 2,), 0, 1 << 20) % (slack + 1)
    sizes = sizes.at[giver].add(-passed).at[receiver].add(passed)
    labels = jnp.searchsorted(jnp.cumsum(sizes), jnp.arange(rows * top), side="right").astype(jnp.int32)
    grid = labels.reshape(top, rows).T
    grid = grid[jax.random.permutation(jax.random.fold_in(own, 1), rows)]
    turn = jax.random.randint(jax.random.fold_in(own, 2), (rows, 1), 0, top)
    return jnp.take_along_axis(grid, (jnp.arange(top)[None, :] + turn) % top, axis=1)


def portions_of(number_of, total, reach, slope, full):
    loads = [(1 << 20) // math.isqrt(rank ** slope) + 1 for rank in range(1, number_of + 1)]
    largest = reach if full else min(reach, max(-(-total // number_of), total * loads[0] // sum(loads)))
    least = 1 if total - largest >= number_of - 1 else 0
    holding, rest = [largest] + [least] * (number_of - 1), total - largest - least * (number_of - 1)
    while rest > 0:
        free = [i for i in range(1, number_of) if holding[i] < largest] or [i for i in range(1, number_of) if holding[i] < reach]
        whole, remaining = sum([loads[i] for i in free]), rest
        for i in free:
            addition = min(reach - holding[i], max(1, remaining * loads[i] // whole), rest)
            holding[i] = holding[i] + addition
            rest = rest - addition
    return np.array(holding)


def scatter_about(stream_key, shape, width, most, pieces=(), kind=jnp.bfloat16):
    values = jax.random.normal(stream_key, shape, jnp.float32) * width
    if len(pieces) > 0:
        values = levels(stream_key, shape, pieces, -0.22, 0.18) * values
    return jnp.clip(values, min=-most, max=most).astype(kind)


def setup_inputs(seed: int = 0) -> dict:
    splits = jax.random.split(jax.random.key(seed), 19)
    new_q = draw_new_q(jax.random.fold_in(splits[18], 71), 0)
    new_k = draw_new_k(jax.random.fold_in(splits[18], 71), 0)
    new_v = scatter_about(splits[2], (REQS, STEPS, D), 1.0, 6.0, ((0, 8),))
    k_cache = draw_k_cache(jax.random.fold_in(splits[18], 71), 0)
    v_cache = scatter_about(splits[4], (POOLS, POOL, PAGE, D), 1.0, 6.0, ((0, 8), (1, 64)))
    lengths = draw_lengths(jax.random.fold_in(splits[18], 71), 0)
    prompt_group = draw_prompt_group(jax.random.fold_in(splits[18], 71), 0)
    prefix_table = draw_prefix_table(jax.random.fold_in(splits[18], 71), 0)
    page_table = draw_page_table(jax.random.fold_in(splits[18], 71), 0)
    rel_bucket = draw_rel_bucket(jax.random.fold_in(splits[18], 71), 0)
    bias_table = scatter_about(splits[10], (BUCKETS, H), 2.0, 8.0, (), jnp.float32)
    hidden_in = draw_hidden_in(jax.random.fold_in(splits[18], 71), 0)
    out_proj = scatter_about(splits[12], (D, D), D ** -0.5, 0.1875, ((1, 64),))
    norm_gain = jnp.clip(1.0 + 0.18 * jax.random.normal(splits[13], (D,), jnp.float32), 0.1, 1.9)
    router_w = scatter_about(splits[14], (D, EXPERTS), D ** -0.5, 0.1875, ((0, 64),), jnp.float32)
    expert_ids_keys = jax.random.split(jax.random.fold_in(splits[15], 1), REQS * STEPS // (REQ_DEV * STEPS))
    expert_ids_turns = jax.random.permutation(jax.random.fold_in(splits[15], 3), REQS * STEPS // (REQ_DEV * STEPS))
    expert_ids = jax.vmap(lambda own, number: assign_block(jax.random.fold_in(splits[15], 2), own, number, REQ_DEV * STEPS, EXPERTS, TOP, MOST, 2))(expert_ids_keys, expert_ids_turns).reshape((REQS, STEPS, TOP))
    w_in = scatter_about(splits[16], (EXPERTS, D, 2, FF), D ** -0.5, 0.1875, ((0, 8), (3, 64)))
    w_down = scatter_about(splits[17], (EXPERTS, FF, D), FF ** -0.5, 0.109375, ((0, 8), (1, 64)))
    return dict(new_q=new_q, new_k=new_k, new_v=new_v, k_cache=k_cache, v_cache=v_cache, lengths=lengths, prompt_group=prompt_group, prefix_table=prefix_table, page_table=page_table, rel_bucket=rel_bucket, bias_table=bias_table, hidden_in=hidden_in, out_proj=out_proj, norm_gain=norm_gain, router_w=router_w, expert_ids=expert_ids, w_in=w_in, w_down=w_down)


def reference(new_q, new_k, new_v, k_cache, v_cache, lengths, prompt_group, prefix_table, page_table, rel_bucket, bias_table, hidden_in, out_proj, norm_gain, router_w, expert_ids, w_in, w_down):
    score_scale = 1.0 / math.sqrt(HD)
    step_ids = jnp.arange(STEPS, dtype=jnp.int32)

    def attend_request(request):
        pool_id = request // REQ_DEV
        page_list = jnp.concatenate([prefix_table[prompt_group[request]], page_table[request]], axis=0)
        safe_pages = jnp.maximum(page_list, 0)
        key_rows = k_cache[pool_id, safe_pages].reshape(MAX_LEN, H, HD).astype(jnp.float32)
        value_rows = v_cache[pool_id, safe_pages].reshape(MAX_LEN, H, HD).astype(jnp.float32)
        length = lengths[request]
        queries = new_q[request].reshape(STEPS, H, HD).astype(jnp.float32)
        key_pos = jnp.arange(MAX_LEN, dtype=jnp.int32)
        query_pos = length + step_ids
        distance = jnp.clip(query_pos[:, None] - key_pos[None, :], 0, MAX_DIST - 1)
        pos_bias = bias_table[rel_bucket[distance]]
        cached = jnp.einsum('shd,lhd->shl', queries, key_rows) * score_scale + jnp.transpose(pos_bias, (0, 2, 1))
        cached = jnp.where((key_pos < length)[None, None, :], cached, -jnp.inf)
        fresh_keys = new_k[request].reshape(STEPS, H, HD).astype(jnp.float32)
        step_gap = step_ids[:, None] - step_ids[None, :]
        fresh_bias = bias_table[rel_bucket[jnp.clip(step_gap, 0, MAX_DIST - 1)]]
        fresh_scores = jnp.einsum('shd,thd->sht', queries, fresh_keys) * score_scale + jnp.transpose(fresh_bias, (0, 2, 1))
        fresh_scores = jnp.where((step_gap >= 0)[:, None, :], fresh_scores, -jnp.inf)
        all_scores = jnp.concatenate([cached, fresh_scores], axis=-1)
        row_top = lax.optimization_barrier(jnp.max(all_scores, axis=-1, keepdims=True))
        weights = jnp.exp(all_scores - row_top)
        weight_total = lax.optimization_barrier(jnp.sum(weights, axis=-1))
        rounded = weights.astype(jnp.bfloat16).astype(jnp.float32)
        all_values = jnp.concatenate([value_rows, new_v[request].reshape(STEPS, H, HD).astype(jnp.float32)], axis=0)
        value_sum = jnp.einsum('shl,lhd->shd', rounded, all_values)
        return (value_sum / weight_total[..., None]).reshape(STEPS, D).astype(jnp.bfloat16)
    attended = lax.map(attend_request, jnp.arange(REQS, dtype=jnp.int32))
    attn_out = jnp.dot(attended.reshape(REQS * STEPS, D), out_proj, preferred_element_type=jnp.float32).astype(jnp.bfloat16)
    residual = hidden_in.reshape(REQS * STEPS, D).astype(jnp.float32) + attn_out.astype(jnp.float32)
    inverse = lax.rsqrt(lax.optimization_barrier(jnp.mean(residual * residual, axis=-1, keepdims=True)) + 1e-06)
    normed_f = residual * norm_gain * inverse
    logits = jnp.dot(normed_f, router_w, precision=lax.Precision.HIGHEST)
    normed = normed_f.astype(jnp.bfloat16)
    chosen_ids = expert_ids.reshape(REQS * STEPS, TOP)
    chosen = jnp.take_along_axis(logits, chosen_ids, axis=1)
    mix_weight = jnp.stack([jax.nn.sigmoid(chosen[:, 0] - chosen[:, 1]), jax.nn.sigmoid(chosen[:, 1] - chosen[:, 0])], axis=1)
    flat_ids = chosen_ids.reshape(-1)
    token_of = jnp.arange(flat_ids.shape[0], dtype=jnp.int32) // TOP
    capacity = N_EXPERT * MOST

    def run_expert(expert):
        expert_hit = flat_ids == expert
        slot_rank = jnp.cumsum(expert_hit.astype(jnp.int32)) - 1
        slot_of = jnp.where(expert_hit, slot_rank, capacity).astype(jnp.int32)
        source_rows = jnp.zeros((capacity,), jnp.int32).at[slot_of].set(token_of, mode='drop')
        rows_in = normed[source_rows]
        preact = jnp.dot(rows_in, w_in[expert].reshape(D, 2 * FF), preferred_element_type=jnp.float32)
        hidden = (jax.nn.gelu(preact[:, :FF]) * preact[:, FF:]).astype(jnp.bfloat16)
        outputs = jnp.dot(hidden, w_down[expert], preferred_element_type=jnp.float32).astype(jnp.bfloat16)
        return (outputs, slot_of)
    expert_outs, slots = lax.map(run_expert, jnp.arange(EXPERTS, dtype=jnp.int32))
    picked_slot = lax.optimization_barrier(jnp.sum(jnp.where(flat_ids[None, :] == jnp.arange(EXPERTS, dtype=jnp.int32)[:, None], slots, 0), axis=0))
    gathered = expert_outs[flat_ids, picked_slot].astype(jnp.float32).reshape(REQS * STEPS, TOP, D)
    moe_out = lax.optimization_barrier(jnp.sum(gathered * mix_weight[..., None], axis=1)).astype(jnp.bfloat16)
    return (attn_out.reshape(REQS, STEPS, D), moe_out.reshape(REQS, STEPS, D))
```

```python
import math

import jax
import jax.numpy as jnp
from jax import lax
from jax.sharding import PartitionSpec as P

MOST = 8
neg_big = -1e30
eps_norm = 1e-06
f32 = jnp.float32
bf16 = jnp.bfloat16


def short(x):
    return lax.reduce_precision(x, 8, 7)


def two_parts(x):
    high = short(x)
    return high, short(x - high)


def body(
    new_q,
    new_k,
    new_v,
    k_cache,
    v_cache,
    lengths,
    prompt_group,
    prefix_table,
    page_table,
    rel_bucket,
    bias_table,
    hidden_in,
    out_proj,
    norm_gain,
    router_w,
    expert_ids,
    w_in,
    w_down,
):
    reqs, steps, width = new_q.shape
    bucket_count, heads = bias_table.shape
    head_size = width // heads
    pages_here, page_len = k_cache.shape[1:3]
    group_rows = prefix_table.shape[0]
    expert_here = w_in.shape[0]
    local = out_proj.shape[1]
    top = expert_ids.shape[2]
    seq_size = lax.axis_size("seq")
    owners = lax.axis_size("expert")
    seq_index = lax.axis_index("seq")
    pool_index = lax.axis_index("expert")
    tokens = reqs * steps
    slots = expert_here * MOST
    rows = owners * slots
    pairs = heads // 2
    lanes = 2 * head_size
    scaling = 1.0 / math.sqrt(head_size)

    with jax.named_scope("positions"):
        local_group = prompt_group - pool_index * group_rows
        prefix_rows = jnp.where(
            (local_group == 0)[:, None], prefix_table[0][None], prefix_table[1][None]
        )
        full_table = jnp.concatenate([prefix_rows, page_table], axis=1)
        page_ids = seq_index * pages_here + jnp.arange(pages_here, dtype=jnp.int32)
        matches = full_table[:, None, :] == page_ids[None, :, None]
        spots = jnp.arange(full_table.shape[1], dtype=jnp.int32)
        logical = jnp.max(jnp.where(matches, spots, -1), axis=2)
        within = jnp.arange(page_len, dtype=jnp.int32)
        key_grid = logical[:, :, None] * page_len + within
        usable = (logical[:, :, None] >= 0) & (key_grid < lengths[:, None, None])
        key_pos = key_grid.reshape(reqs, -1)
        usable = usable.reshape(reqs, -1)
        query_pos = lengths[:, None] + jnp.arange(steps, dtype=jnp.int32)
        distance = query_pos[:, :, None] - key_pos[:, None, :]
        names = jnp.arange(bucket_count + 1, dtype=jnp.int32)
        first_at = jnp.sum((rel_bucket[None, :] < names[:, None]).astype(jnp.int32), axis=1)
        opens = first_at[:-1][:, None, None, None]
        closes = first_at[1:][:, None, None, None]
        onehot = ((distance >= opens) & (distance < closes)).astype(f32)
        pos_bias = jnp.einsum("brsk,bh->hrsk", onehot, bias_table, precision=lax.Precision.HIGHEST)

    with jax.named_scope("local_attention"):
        queries = new_q.reshape(reqs, steps, heads, head_size)
        keys_here = k_cache[0].reshape(-1, heads, head_size)
        values_here = v_cache[0].reshape(-1, heads, head_size)
        scores = jnp.einsum("rshd,khd->hrsk", queries, keys_here, preferred_element_type=f32)
        scores = jnp.where(usable[None, :, None, :], scores * scaling + pos_bias, neg_big)
        part_top = short(jnp.max(scores, axis=-1))
        weights = jnp.where(
            usable[None, :, None, :], jnp.exp(scores - part_top[..., None]), 0.0
        )
        part_total = jnp.sum(weights, axis=-1)
        part_sum = jnp.einsum(
            "hrsk,khd->hrsd", weights.astype(bf16), values_here, preferred_element_type=f32
        )
        total_high, total_low = two_parts(part_total)
        stacked = jnp.stack(
            [part_top, total_high, total_low, jnp.zeros_like(part_top)], axis=-1
        )
        extra = jnp.repeat(stacked.astype(bf16), head_size // 4, axis=-1)
        both = jnp.concatenate([part_sum.astype(bf16), extra], axis=2)
        both = both.reshape(pairs, 2, reqs, 2 * steps, head_size)
        outgoing = jnp.transpose(both, (0, 2, 3, 1, 4)).reshape(seq_size, 2 * steps, lanes)

    with jax.named_scope("exchange_parts"):
        parts = lax.all_to_all(outgoing, "seq", split_axis=0, concat_axis=0, tiled=True)

    with jax.named_scope("combine_parts"):
        my_pair = seq_index // reqs
        my_req = seq_index % reqs
        lane = jnp.arange(lanes, dtype=jnp.int32)
        lane_head = lane // head_size
        quarter = head_size // 4
        from_top = (lane[:, None] == lane_head[None, :] * head_size).astype(bf16)
        from_high = lane[:, None] == lane_head[None, :] * head_size + quarter
        from_low = lane[:, None] == lane_head[None, :] * head_size + 2 * quarter
        from_total = (from_high | from_low).astype(bf16)
        sums = parts[:, :steps].astype(f32)
        extras = parts[:, steps:].reshape(seq_size * steps, lanes)
        tops = jnp.dot(extras, from_top, preferred_element_type=f32)
        totals = jnp.dot(extras, from_total, preferred_element_type=f32)
        tops = tops.reshape(seq_size, steps, lanes)
        totals = totals.reshape(seq_size, steps, lanes)

        def mine(x):
            return lax.dynamic_slice(
                x, (my_req, 0, my_pair * lanes), (1, steps, lanes)
            )[0].astype(f32)

        fresh_q, fresh_k, fresh_v = mine(new_q), mine(new_k), mine(new_v)
        same_head = (lane_head[:, None] == lane_head[None, :]).astype(f32)
        products = fresh_q[:, None, :] * fresh_k[None, :, :]
        fresh_scores = jnp.dot(
            products.reshape(steps * steps, lanes), same_head, precision=lax.Precision.HIGHEST
        ).reshape(steps, steps, lanes)
        near_bias = lax.dynamic_slice(bias_table, (0, my_pair * 2), (steps, 2))
        near_bias = jnp.repeat(near_bias, head_size, axis=1)
        step_ids = jnp.arange(steps, dtype=jnp.int32)
        gap = step_ids[:, None] - step_ids[None, :]
        fresh_bias = sum(
            jnp.where((gap == g)[..., None], near_bias[g], 0.0) for g in range(steps)
        )
        causal = (gap >= 0)[..., None]
        fresh_scores = jnp.where(causal, fresh_scores * scaling + fresh_bias, neg_big)
        peak = jnp.maximum(jnp.max(tops, axis=0), jnp.max(fresh_scores, axis=1))
        factor = jnp.exp(tops - peak)
        fresh_weights = jnp.where(causal, jnp.exp(fresh_scores - peak[:, None, :]), 0.0)
        total = jnp.sum(totals * factor, axis=0) + jnp.sum(fresh_weights, axis=1)
        value_sum = jnp.sum(sums * factor, axis=0) + jnp.sum(
            short(fresh_weights) * fresh_v[None], axis=1
        )
        attended = (value_sum / total).astype(bf16)

    with jax.named_scope("share_attended"):
        shared = jnp.broadcast_to(attended[None], (seq_size, steps, lanes))
        heard = lax.all_to_all(shared, "seq", split_axis=0, concat_axis=0, tiled=True)

    with jax.named_scope("project"):
        heard = heard.reshape(pairs, tokens, lanes)
        attn_flat = jnp.einsum(
            "ptd,pdn->tn",
            heard,
            out_proj.reshape(pairs, lanes, local),
            preferred_element_type=f32,
        ).astype(bf16)
        attn_out = attn_flat.reshape(reqs, steps, local)
        residual = hidden_in.reshape(tokens, local).astype(f32) + attn_flat.astype(f32)
        gained = residual * norm_gain
        squares = jnp.sum(residual * residual, axis=1)
        part_logits = jnp.dot(gained, router_w, precision=lax.Precision.HIGHEST)

    with jax.named_scope("route"):
        chosen_ids = expert_ids.reshape(tokens, top)
        total_experts = owners * expert_here
        expert_names = jnp.arange(total_experts, dtype=jnp.int32)
        flat_ids = chosen_ids.reshape(-1)
        expert_hit = (flat_ids[:, None] == expert_names[None, :]).astype(jnp.int32)
        order = jnp.arange(tokens * top, dtype=jnp.int32)
        earlier = (order[:, None] > order[None, :]) & (flat_ids[:, None] == flat_ids[None, :])
        slot_rank = jnp.sum(earlier.astype(jnp.int32), axis=1)
        dest_row = flat_ids * MOST + slot_rank
        route = (
            dest_row[None, :] == jnp.arange(rows, dtype=jnp.int32)[:, None]
        ).astype(bf16)
        signed_hit = (
            (chosen_ids[:, :1] == expert_names).astype(f32)
            - (chosen_ids[:, 1:] == expert_names).astype(f32)
        )
        lead = jnp.sum(part_logits * signed_hit, axis=1)
        square_high, square_low = two_parts(squares)
        lead_high, lead_low = two_parts(lead)
        ones = jnp.ones_like(lead)
        sides = []
        for sign in (ones, -ones):
            sides.append(
                jnp.concatenate(
                    [
                        gained,
                        jnp.stack(
                            [square_high, square_low, sign * lead_high, sign * lead_low], axis=1
                        ),
                    ],
                    axis=1,
                ).astype(bf16)
            )
        token_rows = jnp.stack(sides, axis=1).reshape(tokens * top, local + 4)
        sent = jnp.dot(route, token_rows, preferred_element_type=f32).astype(bf16)

    with jax.named_scope("to_owners"):
        sent = sent.reshape(owners, slots, local + 4)
        got = lax.all_to_all(sent, "expert", split_axis=0, concat_axis=0, tiled=True)

    with jax.named_scope("share_rows"):
        turned = jnp.pad(got.reshape(rows, local + 4).T, ((0, 4), (0, 0)))
        shared_rows = jnp.broadcast_to(turned[None], (seq_size, local + 8, rows))
        all_rows = lax.all_to_all(shared_rows, "seq", split_axis=0, concat_axis=0, tiled=True)

    with jax.named_scope("experts"):
        features = all_rows[:, :local].reshape(width, rows)
        sides = jnp.sum(all_rows[:, local : local + 4].astype(f32), axis=0)
        inverse = lax.rsqrt((sides[0] + sides[1]) / width + eps_norm)
        mix = jax.nn.sigmoid((sides[2] + sides[3]) * inverse)
        preact = jnp.einsum("edgf,dr->egfr", w_in, features, preferred_element_type=f32) * inverse
        owner_of = jnp.arange(rows, dtype=jnp.int32) // MOST % expert_here
        here = owner_of[None, :] == jnp.arange(expert_here, dtype=jnp.int32)[:, None]
        hidden = jax.nn.gelu(preact[:, 0]) * preact[:, 1]
        hidden = jnp.where(here[:, None, :], hidden, 0.0).astype(bf16)
        part_out = jnp.einsum("efd,efr->dr", w_down, hidden, preferred_element_type=f32)
        part_out = (part_out * mix).astype(bf16).reshape(seq_size, local, rows)

    with jax.named_scope("sum_hidden_units"):
        pieces = lax.all_to_all(part_out, "seq", split_axis=0, concat_axis=0, tiled=True)
        processed = jnp.sum(pieces.astype(f32), axis=0).astype(bf16)

    with jax.named_scope("to_tokens"):
        back = processed.T.reshape(owners, slots, local)
        returned = lax.all_to_all(back, "expert", split_axis=0, concat_axis=0, tiled=True)
        token_route = jnp.sum(route.reshape(rows, tokens, top), axis=2)
        moe_out = jnp.einsum(
            "rt,rd->td", token_route, returned.reshape(rows, local), preferred_element_type=f32
        )
        moe_out = moe_out.astype(bf16).reshape(reqs, steps, local)
    return (attn_out, moe_out)


def solution(mesh):
    return jax.shard_map(
        body,
        mesh=mesh,
        in_specs=(
            P("expert", None, None),
            P("expert", None, None),
            P("expert", None, None),
            P("expert", "seq", None, None),
            P("expert", "seq", None, None),
            P("expert"),
            P("expert"),
            P("expert", None),
            P("expert", None),
            P(),
            P(),
            P("expert", None, "seq"),
            P(None, "seq"),
            P("seq"),
            P("seq", None),
            P("expert", None, None),
            P("expert", None, None, "seq"),
            P("expert", "seq", None),
        ),
        out_specs=(P("expert", None, "seq"), P("expert", None, "seq")),
        check_vma=False,
    )
```

```python
import math

import jax
import jax.numpy as jnp
from jax import lax
from jax.sharding import PartitionSpec as P

MOST = 8
neg_big = -1e30
eps_norm = 1e-06
f32 = jnp.float32
bf16 = jnp.bfloat16


def short(x):
    return lax.reduce_precision(x, 8, 7)


def two_parts(x):
    high = short(x)
    return high, short(x - high)


def body(
    new_q,
    new_k,
    new_v,
    k_cache,
    v_cache,
    lengths,
    prompt_group,
    prefix_table,
    page_table,
    rel_bucket,
    bias_table,
    hidden_in,
    out_proj,
    norm_gain,
    router_w,
    expert_ids,
    w_in,
    w_down,
):
    reqs, steps, width = new_q.shape
    bucket_count, heads = bias_table.shape
    head_size = width // heads
    pages_here, page_len = k_cache.shape[1:3]
    group_rows = prefix_table.shape[0]
    expert_here = w_in.shape[0]
    local = out_proj.shape[1]
    top = expert_ids.shape[2]
    seq_size = lax.axis_size("seq")
    owners = lax.axis_size("expert")
    seq_index = lax.axis_index("seq")
    pool_index = lax.axis_index("expert")
    tokens = reqs * steps
    slots = expert_here * MOST
    rows = owners * slots
    pairs = heads // 2
    lanes = 2 * head_size
    scaling = 1.0 / math.sqrt(head_size)

    with jax.named_scope("positions"):
        local_group = prompt_group - pool_index * group_rows
        prefix_rows = jnp.where(
            (local_group == 0)[:, None], prefix_table[0][None], prefix_table[1][None]
        )
        full_table = jnp.concatenate([prefix_rows, page_table], axis=1)
        page_ids = seq_index * pages_here + jnp.arange(pages_here, dtype=jnp.int32)
        matches = full_table[:, None, :] == page_ids[None, :, None]
        spots = jnp.arange(full_table.shape[1], dtype=jnp.int32)
        logical = jnp.max(jnp.where(matches, spots, -1), axis=2)
        within = jnp.arange(page_len, dtype=jnp.int32)
        key_grid = logical[:, :, None] * page_len + within
        usable = (logical[:, :, None] >= 0) & (key_grid < lengths[:, None, None])
        key_pos = key_grid.reshape(reqs, -1)
        usable = usable.reshape(reqs, -1)
        query_pos = lengths[:, None] + jnp.arange(steps, dtype=jnp.int32)
        distance = query_pos[:, :, None] - key_pos[:, None, :]
        names = jnp.arange(bucket_count + 1, dtype=jnp.int32)
        first_at = jnp.sum((rel_bucket[None, :] < names[:, None]).astype(jnp.int32), axis=1)
        opens = first_at[:-1][:, None, None, None]
        closes = first_at[1:][:, None, None, None]
        onehot = ((distance >= opens) & (distance < closes)).astype(f32)
        pos_bias = jnp.einsum("brsk,bh->hrsk", onehot, bias_table, precision=lax.Precision.HIGHEST)

    with jax.named_scope("local_attention"):
        queries = new_q.reshape(reqs, steps, heads, head_size)
        keys_here = k_cache[0].reshape(-1, heads, head_size)
        values_here = v_cache[0].reshape(-1, heads, head_size)
        scores = jnp.einsum("rshd,khd->hrsk", queries, keys_here, preferred_element_type=f32)
        scores = jnp.where(usable[None, :, None, :], scores * scaling + pos_bias, neg_big)
        part_top = short(jnp.max(scores, axis=-1))
        weights = jnp.where(
            usable[None, :, None, :], jnp.exp(scores - part_top[..., None]), 0.0
        )
        part_total = jnp.sum(weights, axis=-1)
        part_sum = jnp.einsum(
            "hrsk,khd->hrsd", weights.astype(bf16), values_here, preferred_element_type=f32
        )
        total_high, total_low = two_parts(part_total)
        stacked = jnp.stack(
            [part_top, total_high, total_low, jnp.zeros_like(part_top)], axis=-1
        )
        extra = jnp.repeat(stacked.astype(bf16), head_size // 4, axis=-1)
        both = jnp.concatenate([part_sum.astype(bf16), extra], axis=2)
        both = both.reshape(pairs, 2, reqs, 2 * steps, head_size)
        outgoing = jnp.transpose(both, (0, 2, 3, 1, 4)).reshape(seq_size, 2 * steps, lanes)

    with jax.named_scope("exchange_parts"):
        parts = lax.all_to_all(outgoing, "seq", split_axis=0, concat_axis=0, tiled=True)

    with jax.named_scope("combine_parts"):
        my_pair = seq_index // reqs
        my_req = seq_index % reqs
        lane = jnp.arange(lanes, dtype=jnp.int32)
        lane_head = lane // head_size
        quarter = head_size // 4
        from_top = (lane[:, None] == lane_head[None, :] * head_size).astype(bf16)
        from_high = lane[:, None] == lane_head[None, :] * head_size + quarter
        from_low = lane[:, None] == lane_head[None, :] * head_size + 2 * quarter
        from_total = (from_high | from_low).astype(bf16)
        sums = parts[:, :steps].astype(f32)
        extras = parts[:, steps:].reshape(seq_size * steps, lanes)
        tops = jnp.dot(extras, from_top, preferred_element_type=f32)
        totals = jnp.dot(extras, from_total, preferred_element_type=f32)
        tops = tops.reshape(seq_size, steps, lanes)
        totals = totals.reshape(seq_size, steps, lanes)

        def mine(x):
            return lax.dynamic_slice(
                x, (my_req, 0, my_pair * lanes), (1, steps, lanes)
            )[0].astype(f32)

        fresh_q, fresh_k, fresh_v = mine(new_q), mine(new_k), mine(new_v)
        same_head = (lane_head[:, None] == lane_head[None, :]).astype(f32)
        products = fresh_q[:, None, :] * fresh_k[None, :, :]
        fresh_scores = jnp.dot(
            products.reshape(steps * steps, lanes), same_head, precision=lax.Precision.HIGHEST
        ).reshape(steps, steps, lanes)
        near_bias = lax.dynamic_slice(bias_table, (0, my_pair * 2), (steps, 2))
        near_bias = jnp.repeat(near_bias, head_size, axis=1)
        step_ids = jnp.arange(steps, dtype=jnp.int32)
        gap = step_ids[:, None] - step_ids[None, :]
        fresh_bias = sum(
            jnp.where((gap == g)[..., None], near_bias[g], 0.0) for g in range(steps)
        )
        causal = (gap >= 0)[..., None]
        fresh_scores = jnp.where(causal, fresh_scores * scaling + fresh_bias, neg_big)
        peak = jnp.maximum(jnp.max(tops, axis=0), jnp.max(fresh_scores, axis=1))
        factor = jnp.exp(tops - peak)
        fresh_weights = jnp.where(causal, jnp.exp(fresh_scores - peak[:, None, :]), 0.0)
        total = jnp.sum(totals * factor, axis=0) + jnp.sum(fresh_weights, axis=1)
        value_sum = jnp.sum(sums * factor, axis=0) + jnp.sum(
            short(fresh_weights) * fresh_v[None], axis=1
        )
        attended = (value_sum / total).astype(bf16)

    with jax.named_scope("share_attended"):
        shared = jnp.broadcast_to(attended[None], (seq_size, steps, lanes))
        heard = lax.all_to_all(shared, "seq", split_axis=0, concat_axis=0, tiled=True)

    with jax.named_scope("project"):
        heard = heard.reshape(pairs, tokens, lanes)
        attn_flat = jnp.einsum(
            "ptd,pdn->tn",
            heard,
            out_proj.reshape(pairs, lanes, local),
            preferred_element_type=f32,
        ).astype(bf16)
        attn_out = attn_flat.reshape(reqs, steps, local)
        residual = hidden_in.reshape(tokens, local).astype(f32) + attn_flat.astype(f32)
        gained = residual * norm_gain
        squares = jnp.sum(residual * residual, axis=1)
        part_logits = jnp.dot(gained, router_w, precision=lax.Precision.HIGHEST)

    with jax.named_scope("route"):
        chosen_ids = expert_ids.reshape(tokens, top)
        total_experts = owners * expert_here
        expert_names = jnp.arange(total_experts, dtype=jnp.int32)
        flat_ids = chosen_ids.reshape(-1)
        expert_hit = (flat_ids[:, None] == expert_names[None, :]).astype(jnp.int32)
        order = jnp.arange(tokens * top, dtype=jnp.int32)
        earlier = (order[:, None] > order[None, :]) & (flat_ids[:, None] == flat_ids[None, :])
        slot_rank = jnp.sum(earlier.astype(jnp.int32), axis=1)
        dest_row = flat_ids * MOST + slot_rank
        dest_pair = dest_row.reshape(tokens, top)
        route = (
            dest_row[None, :] == jnp.arange(rows, dtype=jnp.int32)[:, None]
        ).astype(bf16)
        signed_hit = (
            (chosen_ids[:, :1] == expert_names).astype(f32)
            - (chosen_ids[:, 1:] == expert_names).astype(f32)
        )
        lead = jnp.sum(part_logits * signed_hit, axis=1)
        square_high, square_low = two_parts(squares)
        lead_high, lead_low = two_parts(lead)
        ones = jnp.ones_like(lead)
        sides = []
        for sign in (ones, -ones):
            sides.append(
                jnp.concatenate(
                    [
                        gained,
                        jnp.stack(
                            [square_high, square_low, sign * lead_high, sign * lead_low], axis=1
                        ),
                        jnp.zeros((tokens, lanes - local - 4), f32),
                    ],
                    axis=1,
                ).astype(bf16)
            )
        token_rows = jnp.stack(sides, axis=1).reshape(tokens * top, lanes)
        sent = jnp.dot(route, token_rows, preferred_element_type=f32).astype(bf16)

    with jax.named_scope("to_owners"):
        sent = sent.reshape(owners, slots, lanes)
        sent, first_rows, second_rows = lax.optimization_barrier(
            (sent, dest_pair[:, 0], dest_pair[:, 1])
        )
        got = lax.all_to_all(sent, "expert", split_axis=0, concat_axis=0, tiled=True)
        row_names = jnp.arange(rows, dtype=jnp.int32)[:, None]
        first_route = (row_names == first_rows[None, :]).astype(bf16)
        got, first_route = lax.optimization_barrier((got, first_route))

    with jax.named_scope("share_rows"):
        turned = got.reshape(rows, lanes)[:, : local + 8].T
        shared_rows = jnp.broadcast_to(turned[None], (seq_size, local + 8, rows))
        all_rows = lax.all_to_all(shared_rows, "seq", split_axis=0, concat_axis=0, tiled=True)

    with jax.named_scope("experts"):
        features = all_rows[:, :local].reshape(width, rows)
        sides = jnp.sum(all_rows[:, local : local + 4].astype(f32), axis=0)
        inverse = lax.rsqrt((sides[0] + sides[1]) / width + eps_norm)
        mix = jax.nn.sigmoid((sides[2] + sides[3]) * inverse)
        preact = jnp.einsum("edgf,dr->egfr", w_in, features, preferred_element_type=f32) * inverse
        owner_of = jnp.arange(rows, dtype=jnp.int32) // MOST % expert_here
        here = owner_of[None, :] == jnp.arange(expert_here, dtype=jnp.int32)[:, None]
        hidden = jax.nn.gelu(preact[:, 0]) * preact[:, 1]
        hidden = jnp.where(here[:, None, :], hidden, 0.0).astype(bf16)
        part_out = jnp.einsum("efd,efr->dr", w_down, hidden, preferred_element_type=f32)
        part_out = (part_out * mix).astype(bf16).reshape(seq_size, local, rows)

    with jax.named_scope("sum_hidden_units"):
        part_out, second_rows = lax.optimization_barrier((part_out, second_rows))
        pieces = lax.all_to_all(part_out, "seq", split_axis=0, concat_axis=0, tiled=True)
        token_route = first_route + (row_names == second_rows[None, :]).astype(bf16)
        pieces, token_route = lax.optimization_barrier((pieces, token_route))
        processed = jnp.sum(pieces.astype(f32), axis=0).astype(bf16)

    with jax.named_scope("to_tokens"):
        back = processed.T.reshape(owners, slots, local)
        returned = lax.all_to_all(back, "expert", split_axis=0, concat_axis=0, tiled=True)
        moe_out = jnp.einsum(
            "rt,rd->td", token_route, returned.reshape(rows, local), preferred_element_type=f32
        )
        moe_out = moe_out.astype(bf16).reshape(reqs, steps, local)
    return (attn_out, moe_out)


def solution(mesh):
    return jax.shard_map(
        body,
        mesh=mesh,
        in_specs=(
            P("expert", None, None),
            P("expert", None, None),
            P("expert", None, None),
            P("expert", "seq", None, None),
            P("expert", "seq", None, None),
            P("expert"),
            P("expert"),
            P("expert", None),
            P("expert", None),
            P(),
            P(),
            P("expert", None, "seq"),
            P(None, "seq"),
            P("seq"),
            P("seq", None),
            P("expert", None, None),
            P("expert", None, None, "seq"),
            P("expert", "seq", None),
        ),
        out_specs=(P("expert", None, "seq"), P("expert", None, "seq")),
        check_vma=False,
    )
```

```python
import math

import jax
import jax.numpy as jnp
from jax import lax
from jax.sharding import PartitionSpec as P

MOST = 8
neg_big = -1e30
eps_norm = 1e-06
f32 = jnp.float32
bf16 = jnp.bfloat16


def short(x):
    return lax.reduce_precision(x, 8, 7)


def two_parts(x):
    high = short(x)
    return high, short(x - high)


def body(
    new_q,
    new_k,
    new_v,
    k_cache,
    v_cache,
    lengths,
    prompt_group,
    prefix_table,
    page_table,
    rel_bucket,
    bias_table,
    hidden_in,
    out_proj,
    norm_gain,
    router_w,
    expert_ids,
    w_in,
    w_down,
):
    reqs, steps, width = new_q.shape
    bucket_count, heads = bias_table.shape
    head_size = width // heads
    pages_here, page_len = k_cache.shape[1:3]
    group_rows = prefix_table.shape[0]
    expert_here = w_in.shape[0]
    local = out_proj.shape[1]
    top = expert_ids.shape[2]
    seq_size = lax.axis_size("seq")
    owners = lax.axis_size("expert")
    seq_index = lax.axis_index("seq")
    pool_index = lax.axis_index("expert")
    tokens = reqs * steps
    slots = expert_here * MOST
    rows = owners * slots
    pairs = heads // 2
    lanes = 2 * head_size
    scaling = 1.0 / math.sqrt(head_size)

    with jax.named_scope("positions"):
        local_group = prompt_group - pool_index * group_rows
        prefix_rows = jnp.where(
            (local_group == 0)[:, None], prefix_table[0][None], prefix_table[1][None]
        )
        full_table = jnp.concatenate([prefix_rows, page_table], axis=1)
        page_ids = seq_index * pages_here + jnp.arange(pages_here, dtype=jnp.int32)
        matches = full_table[:, None, :] == page_ids[None, :, None]
        spots = jnp.arange(full_table.shape[1], dtype=jnp.int32)
        logical = jnp.max(jnp.where(matches, spots, -1), axis=2)
        within = jnp.arange(page_len, dtype=jnp.int32)
        key_grid = logical[:, :, None] * page_len + within
        usable = (logical[:, :, None] >= 0) & (key_grid < lengths[:, None, None])
        key_pos = key_grid.reshape(reqs, -1)
        usable = usable.reshape(reqs, -1)
        query_pos = lengths[:, None] + jnp.arange(steps, dtype=jnp.int32)
        distance = query_pos[:, :, None] - key_pos[:, None, :]
        names = jnp.arange(bucket_count + 1, dtype=jnp.int32)
        first_at = jnp.sum((rel_bucket[None, :] < names[:, None]).astype(jnp.int32), axis=1)
        opens = first_at[:-1][:, None, None, None]
        closes = first_at[1:][:, None, None, None]
        onehot = ((distance >= opens) & (distance < closes)).astype(f32)
        pos_bias = jnp.einsum("brsk,bh->hrsk", onehot, bias_table, precision=lax.Precision.HIGHEST)

    with jax.named_scope("local_attention"):
        pair_lane = jnp.arange(lanes, dtype=jnp.int32)
        in_second = pair_lane >= head_size
        own_lane = in_second[None, :] == (jnp.arange(2) == 1)[:, None]
        queries = jnp.transpose(new_q.reshape(tokens, pairs, lanes), (1, 0, 2))
        queries = jnp.where(own_lane[None, :, None, :], queries[:, None], 0).astype(bf16)
        queries = queries.reshape(pairs, 2, reqs, steps, lanes)
        keys_here = k_cache[0].reshape(-1, pairs, lanes)
        values_here = v_cache[0].reshape(-1, pairs, lanes)
        allowed = usable[None, None, :, None, :]
        scores = jnp.einsum("pgrsd,kpd->pgrsk", queries, keys_here, preferred_element_type=f32)
        pair_bias = pos_bias.reshape(pairs, 2, reqs, steps, -1)
        scores = jnp.where(allowed, scores * scaling + pair_bias, neg_big)
        part_top = short(jnp.max(scores, axis=-1, keepdims=True))
        weights = jnp.where(allowed, jnp.exp(scores - part_top), 0.0)
        part_total = jnp.sum(weights, axis=-1, keepdims=True)
        part_sum = jnp.einsum(
            "pgrsk,kpd->pgrsd", weights.astype(bf16), values_here, preferred_element_type=f32
        )
        total_high, total_low = two_parts(part_total)
        spot = pair_lane % head_size // (head_size // 4)
        extra = jnp.where(
            spot == 0,
            part_top,
            jnp.where(spot == 1, total_high, jnp.where(spot == 2, total_low, 0.0)),
        )
        mine_sum = jnp.where(in_second, part_sum[:, 1], part_sum[:, 0]).astype(bf16)
        mine_extra = jnp.where(in_second, extra[:, 1], extra[:, 0]).astype(bf16)
        outgoing = jnp.concatenate([mine_sum, mine_extra], axis=-1)
        outgoing = outgoing.reshape(seq_size, steps, 2 * lanes)

    with jax.named_scope("exchange_parts"):
        parts = lax.all_to_all(outgoing, "seq", split_axis=0, concat_axis=0, tiled=True)

    with jax.named_scope("combine_parts"):
        my_pair = seq_index // reqs
        my_req = seq_index % reqs
        lane = jnp.arange(lanes, dtype=jnp.int32)
        lane_head = lane // head_size
        quarter = head_size // 4
        from_top = (lane[:, None] == lane_head[None, :] * head_size).astype(bf16)
        from_high = lane[:, None] == lane_head[None, :] * head_size + quarter
        from_low = lane[:, None] == lane_head[None, :] * head_size + 2 * quarter
        from_total = (from_high | from_low).astype(bf16)
        sums = parts[:, :, :lanes].astype(f32)
        extras = parts[:, :, lanes:].reshape(seq_size * steps, lanes)
        tops = jnp.dot(extras, from_top, preferred_element_type=f32)
        totals = jnp.dot(extras, from_total, preferred_element_type=f32)
        tops = tops.reshape(seq_size, steps, lanes)
        totals = totals.reshape(seq_size, steps, lanes)

        def mine(x):
            return lax.dynamic_slice(
                x, (my_req, 0, my_pair * lanes), (1, steps, lanes)
            )[0].astype(f32)

        fresh_q, fresh_k, fresh_v = mine(new_q), mine(new_k), mine(new_v)
        same_head = (lane_head[:, None] == lane_head[None, :]).astype(f32)
        products = fresh_q[:, None, :] * fresh_k[None, :, :]
        fresh_scores = jnp.dot(
            products.reshape(steps * steps, lanes), same_head, precision=lax.Precision.HIGHEST
        ).reshape(steps, steps, lanes)
        near_bias = lax.dynamic_slice(bias_table, (0, my_pair * 2), (steps, 2))
        near_bias = jnp.repeat(near_bias, head_size, axis=1)
        step_ids = jnp.arange(steps, dtype=jnp.int32)
        gap = step_ids[:, None] - step_ids[None, :]
        fresh_bias = sum(
            jnp.where((gap == g)[..., None], near_bias[g], 0.0) for g in range(steps)
        )
        causal = (gap >= 0)[..., None]
        fresh_scores = jnp.where(causal, fresh_scores * scaling + fresh_bias, neg_big)
        peak = jnp.maximum(jnp.max(tops, axis=0), jnp.max(fresh_scores, axis=1))
        factor = jnp.exp(tops - peak)
        fresh_weights = jnp.where(causal, jnp.exp(fresh_scores - peak[:, None, :]), 0.0)
        total = jnp.sum(totals * factor, axis=0) + jnp.sum(fresh_weights, axis=1)
        value_sum = jnp.sum(sums * factor, axis=0) + jnp.sum(
            short(fresh_weights) * fresh_v[None], axis=1
        )
        attended = (value_sum / total).astype(bf16)

    with jax.named_scope("share_attended"):
        shared = jnp.broadcast_to(attended[None], (seq_size, steps, lanes))
        heard = lax.all_to_all(shared, "seq", split_axis=0, concat_axis=0, tiled=True)

    with jax.named_scope("project"):
        heard = heard.reshape(pairs, tokens, lanes)
        attn_flat = jnp.einsum(
            "ptd,pdn->tn",
            heard,
            out_proj.reshape(pairs, lanes, local),
            preferred_element_type=f32,
        ).astype(bf16)
        attn_out = attn_flat.reshape(reqs, steps, local)
        residual = hidden_in.reshape(tokens, local).astype(f32) + attn_flat.astype(f32)
        gained = residual * norm_gain
        squares = jnp.sum(residual * residual, axis=1)
        part_logits = jnp.dot(gained, router_w, precision=lax.Precision.HIGHEST)

    with jax.named_scope("route"):
        chosen_ids = expert_ids.reshape(tokens, top)
        total_experts = owners * expert_here
        expert_names = jnp.arange(total_experts, dtype=jnp.int32)
        flat_ids = chosen_ids.reshape(-1)
        expert_hit = (flat_ids[:, None] == expert_names[None, :]).astype(jnp.int32)
        order = jnp.arange(tokens * top, dtype=jnp.int32)
        earlier = (order[:, None] > order[None, :]) & (flat_ids[:, None] == flat_ids[None, :])
        slot_rank = jnp.sum(earlier.astype(jnp.int32), axis=1)
        dest_row = flat_ids * MOST + slot_rank
        route = (
            dest_row[None, :] == jnp.arange(rows, dtype=jnp.int32)[:, None]
        ).astype(bf16)
        signed_hit = (
            (chosen_ids[:, :1] == expert_names).astype(f32)
            - (chosen_ids[:, 1:] == expert_names).astype(f32)
        )
        lead = jnp.sum(part_logits * signed_hit, axis=1)
        square_high, square_low = two_parts(squares)
        lead_high, lead_low = two_parts(lead)
        ones = jnp.ones_like(lead)
        sides = []
        for sign in (ones, -ones):
            sides.append(
                jnp.concatenate(
                    [
                        gained,
                        jnp.stack(
                            [square_high, square_low, sign * lead_high, sign * lead_low], axis=1
                        ),
                    ],
                    axis=1,
                ).astype(bf16)
            )
        token_rows = jnp.stack(sides, axis=1).reshape(tokens * top, local + 4)
        sent = jnp.dot(route, token_rows, preferred_element_type=f32).astype(bf16)

    with jax.named_scope("to_owners"):
        sent = sent.reshape(owners, slots, local + 4)
        got = lax.all_to_all(sent, "expert", split_axis=0, concat_axis=0, tiled=True)

    with jax.named_scope("share_rows"):
        turned = jnp.pad(got.reshape(rows, local + 4).T, ((0, 4), (0, 0)))
        shared_rows = jnp.broadcast_to(turned[None], (seq_size, local + 8, rows))
        all_rows = lax.all_to_all(shared_rows, "seq", split_axis=0, concat_axis=0, tiled=True)

    with jax.named_scope("experts"):
        features = all_rows[:, :local].reshape(width, rows)
        sides = jnp.sum(all_rows[:, local : local + 4].astype(f32), axis=0)
        inverse = lax.rsqrt((sides[0] + sides[1]) / width + eps_norm)
        mix = jax.nn.sigmoid((sides[2] + sides[3]) * inverse)
        preact = jnp.einsum("edgf,dr->egfr", w_in, features, preferred_element_type=f32) * inverse
        owner_of = jnp.arange(rows, dtype=jnp.int32) // MOST % expert_here
        here = owner_of[None, :] == jnp.arange(expert_here, dtype=jnp.int32)[:, None]
        hidden = jax.nn.gelu(preact[:, 0]) * preact[:, 1]
        hidden = jnp.where(here[:, None, :], hidden, 0.0).astype(bf16)
        part_out = jnp.einsum("efd,efr->dr", w_down, hidden, preferred_element_type=f32)
        part_out = (part_out * mix).astype(bf16).reshape(seq_size, local, rows)

    with jax.named_scope("sum_hidden_units"):
        pieces = lax.all_to_all(part_out, "seq", split_axis=0, concat_axis=0, tiled=True)
        processed = jnp.sum(pieces.astype(f32), axis=0).astype(bf16)

    with jax.named_scope("to_tokens"):
        back = processed.T.reshape(owners, slots, local)
        returned = lax.all_to_all(back, "expert", split_axis=0, concat_axis=0, tiled=True)
        token_route = jnp.sum(route.reshape(rows, tokens, top), axis=2)
        moe_out = jnp.einsum(
            "rt,rd->td", token_route, returned.reshape(rows, local), preferred_element_type=f32
        )
        moe_out = moe_out.astype(bf16).reshape(reqs, steps, local)
    return (attn_out, moe_out)


def solution(mesh):
    return jax.shard_map(
        body,
        mesh=mesh,
        in_specs=(
            P("expert", None, None),
            P("expert", None, None),
            P("expert", None, None),
            P("expert", "seq", None, None),
            P("expert", "seq", None, None),
            P("expert"),
            P("expert"),
            P("expert", None),
            P("expert", None),
            P(),
            P(),
            P("expert", None, "seq"),
            P(None, "seq"),
            P("seq"),
            P("seq", None),
            P("expert", None, None),
            P("expert", None, None, "seq"),
            P("expert", "seq", None),
        ),
        out_specs=(P("expert", None, "seq"), P("expert", None, "seq")),
        check_vma=False,
    )
```
